32 devices in a mesh: groups: 2 (over y), nodes: 16 (over z, x, core).
Axes of the slice: x: 2, y: 2, z: 4, core: 2. Of those that a mesh axis runs over, the one named last changes fastest.
Arguments:
- queries: bfloat16 [4096, 2048], P(('groups', 'nodes')), parts along dimension 0, may hold values from -192 to 192
- seg_kv: bfloat16 [2, 4096, 1024], P(None, ('groups', 'nodes')), parts along dimension 1, may hold values from -6 to 6
- kv_store: bfloat16 [2, 864, 128, 1024], P(None, ('groups', 'nodes')), parts along dimension 1, may hold values from -6 to 6
- seg_parent: int32 [8], P('groups'), parts along dimension 0, may hold values from 0 to 39, as said below
- block_up: int32 [80], P('groups'), parts along dimension 0, may hold values from -1 to 12, as said below
- page_owner: int32 [80, 4], P('groups'), parts along dimension 0, may hold values from 0 to 15, as said below
- page_slot: int32 [80, 4], P('groups'), parts along dimension 0, may hold values from 0 to 26, as said below
Outputs:
- attended: bfloat16 [4096, 2048], P(('groups', 'nodes')), parts along dimension 0
The draws below stay inside these ranges and needn't reach their ends.
There are 2 independent parts, one for each index of `groups`. The reference program is written for one: setup_inputs(seed, part) draws one part's arguments, and reference() takes and returns one part's arrays. A program takes and returns all parts, laid end to end along the dimension named above; each array names one. Nothing has to cross between parts.
Inputs may be any that keep to these rules, and one draw needn't show every extreme that they name: `block_up`: block 0 is the root and alone has -1; every other block's parent has a smaller number and lies one depth above it; depth d holds 3**d blocks, numbered in order of depth. `seg_parent`: some segment's parent is the last block, at depth 4 - 1, so that its path holds 4 blocks. `page_owner`: the pages of the blocks on one segment's path lie on distinct devices, so a device needs at most one page from each device, and some device needs one from every device; a device holds at most 27 pages, and some device holds 27. `page_slot`: no two pages share a device and a slot.
All inputs are finite; a program needn't handle non-finite values.
Results may differ from the reference program's by a relative error of at most 0.0035.
Values may be sent and summed in bfloat16 or wider, within the bound.
No kernel may reach another device: no remote copies, remote signals or barrier semaphores. Data moves between devices by JAX's collectives and lax.ppermute only.
A program may use at most 64 MiB of HBM per device.

```python
import jax
import jax.numpy as jnp
import numpy as np
from jax import lax

HEADS = 16
KV_HEADS = 8
HEAD_DIM = 128
DEPTHS = 4
BRANCH = 3
BLOCK = 512
SEGS = 4
TOKENS = 2048
NBLK = 40
SLOTS = 27
PAGES = 4
PAGE_TOK = 128
N_NODES = 16


def tree_tables(key):
    key = jax.random.fold_in(key, 11)
    key_up, key_depth, key_pick, key_force, key_perm, key_rot, key_slot = jax.random.split(key, 7)
    level_size = np.array([BRANCH ** depth_step for depth_step in range(DEPTHS)], np.int32)
    level_start = np.array([(BRANCH ** depth_step - 1) // (BRANCH - 1) for depth_step in range(DEPTHS)], np.int32)
    block_depth = np.concatenate([np.full(BRANCH ** depth_step, depth_step, np.int32) for depth_step in range(DEPTHS)])
    level_place = np.concatenate([np.arange(BRANCH ** depth_step, dtype=np.int32) for depth_step in range(DEPTHS)])
    upper_depth = np.maximum(block_depth - 1, 0)
    last_in_level = level_place == level_size[block_depth] - 1
    raw_up = jax.random.randint(key_up, (NBLK,), 0, 1 << 30)
    block_up = jnp.asarray(level_start[upper_depth]) + raw_up % jnp.asarray(level_size[upper_depth])
    block_up = jnp.where(jnp.asarray(last_in_level), jnp.asarray(level_start[block_depth] - 1), block_up)
    block_up = jnp.where(jnp.asarray(block_depth) > 0, block_up, -1).astype(jnp.int32)
    seg_depth = jax.random.randint(key_depth, (SEGS,), 0, DEPTHS)
    forced = jax.random.randint(key_force, (), 0, SEGS)
    raw_pick = jax.random.randint(key_pick, (SEGS,), 0, 1 << 30)
    seg_parent = jnp.asarray(level_start)[seg_depth] + raw_pick % jnp.asarray(level_size)[seg_depth]
    seg_parent = jnp.where(jnp.arange(SEGS) == forced, NBLK - 1, seg_parent)
    shuffle = jax.random.permutation(key_perm, N_NODES).astype(jnp.int32)
    rotation = jax.random.randint(key_rot, (NBLK, 1), 0, PAGES)
    band_place = jnp.asarray(block_depth)[:, None] * PAGES + (jnp.arange(PAGES)[None, :] + rotation) % PAGES
    page_owner = shuffle[band_place]
    slot_keys = jax.random.split(key_slot, N_NODES)
    owner_order = jax.vmap(lambda one_key: jax.random.permutation(one_key, SLOTS))(slot_keys)
    page_slot = owner_order[page_owner, jnp.asarray(level_place)[:, None]]
    return (seg_parent.astype(jnp.int32), block_up, page_owner.astype(jnp.int32), page_slot.astype(jnp.int32))


def attention_inputs(key):
    key = jax.random.fold_in(key, 29)
    key_query, key_pair = jax.random.split(key, 2)
    kv_width = KV_HEADS * HEAD_DIM
    queries = 2.0 * jax.random.normal(key_query, (TOKENS, HEADS * HEAD_DIM), jnp.float32)
    kv_pairs = jax.random.normal(key_pair, (2, TOKENS, kv_width), jnp.float32)
    queries = jnp.clip(queries, -192.0, 192.0).astype(jnp.bfloat16)
    kv_pairs = jnp.clip(kv_pairs, -6.0, 6.0).astype(jnp.bfloat16)
    return (queries, kv_pairs)


def draw_queries(key, part):
    return attention_inputs(key)[0]


def draw_seg_kv(key, part):
    return attention_inputs(key)[1]


def draw_seg_parent(key, part):
    return tree_tables(key)[0]


def draw_block_up(key, part):
    return tree_tables(key)[1]


def draw_page_owner(key, part):
    return tree_tables(key)[2]


def draw_page_slot(key, part):
    return tree_tables(key)[3]


def level_of(rng, dims, shards, least, high):
    def one(axis_at, parts):
        heights = jax.random.uniform(jax.random.fold_in(jax.random.fold_in(rng, 6), axis_at), (parts,), jnp.float32, least / len(shards), high / len(shards))
        return jnp.repeat(jnp.exp(heights), dims[axis_at] // parts).reshape((-1,) + (1,) * (len(dims) - axis_at - 1))

    gain = one(*shards[0])
    for cut in shards[1:]:
        gain = gain * one(*cut)
    return gain


def normal_values(own_key, extent, spread, most, shards=(), kind=jnp.bfloat16):
    loudness = level_of(own_key, extent, shards, -0.22, 0.18) if shards else 1.0
    entries = jax.random.normal(own_key, extent, jnp.float32) * spread * loudness
    return jnp.minimum(jnp.maximum(entries, -most), most).astype(kind)


def setup_inputs(seed: int = 0, part: int = 0) -> dict:
    arg_keys = jax.random.split(jax.random.key(seed), 8)
    own_keys = jax.random.split(jax.random.fold_in(arg_keys[7], part), 8)
    queries = draw_queries(jax.random.fold_in(jax.random.fold_in(arg_keys[7], part), 71), part)
    seg_kv = draw_seg_kv(jax.random.fold_in(jax.random.fold_in(arg_keys[7], part), 71), part)
    kv_store = normal_values(own_keys[2], (2, N_NODES * SLOTS, PAGE_TOK, KV_HEADS * HEAD_DIM), 1.0, 6.0, ((1, 16),))
    seg_parent = draw_seg_parent(jax.random.fold_in(jax.random.fold_in(arg_keys[7], part), 71), part)
    block_up = draw_block_up(jax.random.fold_in(jax.random.fold_in(arg_keys[7], part), 71), part)
    page_owner = draw_page_owner(jax.random.fold_in(jax.random.fold_in(arg_keys[7], part), 71), part)
    page_slot = draw_page_slot(jax.random.fold_in(jax.random.fold_in(arg_keys[7], part), 71), part)
    return dict(queries=queries, seg_kv=seg_kv, kv_store=kv_store, seg_parent=seg_parent, block_up=block_up, page_owner=page_owner, page_slot=page_slot)


query_scale = 168.0 ** -0.5


def walk_paths(seg_parent, block_up):
    chain_list = []
    current = seg_parent
    for depth_step in range(DEPTHS):
        chain_list.append(current)
        safe_blocks = jnp.maximum(current, 0).astype(jnp.int32)
        current = jnp.where(current >= 0, block_up[safe_blocks], -1).astype(jnp.int32)
    return jnp.stack(chain_list, axis=1)


def reference(queries, seg_kv, kv_store, seg_parent, block_up, page_owner, page_slot):
    path_blocks = walk_paths(seg_parent, block_up)
    head_group = HEADS // KV_HEADS
    kv_width = KV_HEADS * HEAD_DIM
    positions = jnp.arange(BLOCK)
    own_live = positions[None, :] <= positions[:, None]

    def one_segment(segment):
        blocks = path_blocks[segment]
        path_live = blocks >= 0
        safe_blocks = jnp.maximum(blocks, 0).astype(jnp.int32)
        store_rows = (page_owner[safe_blocks] * SLOTS + page_slot[safe_blocks]).reshape(-1).astype(jnp.int32)
        ancestors = jnp.take(kv_store, store_rows, axis=1).reshape(2, DEPTHS * BLOCK, kv_width)
        anc_live = jnp.repeat(path_live, BLOCK)
        row_start = (segment * BLOCK).astype(jnp.int32)
        own_kv = lax.dynamic_slice_in_dim(seg_kv, row_start, BLOCK, 1)
        all_kv = jnp.concatenate([own_kv, ancestors], axis=1).astype(jnp.float32)
        visible = jnp.concatenate([own_live, jnp.broadcast_to(anc_live[None, :], (BLOCK, DEPTHS * BLOCK))], axis=1)
        query_rows = lax.dynamic_slice_in_dim(queries, row_start, BLOCK, 0).astype(jnp.float32)
        query_rows = query_rows.reshape(BLOCK, KV_HEADS, head_group, HEAD_DIM)
        key_rows = all_kv[0].reshape(-1, KV_HEADS, HEAD_DIM)
        value_rows = all_kv[1].reshape(-1, KV_HEADS, HEAD_DIM)
        scores = jnp.einsum("tkgd,nkd->tkgn", query_rows, key_rows) * query_scale
        scores = jnp.where(visible[:, None, None, :], scores, -jnp.inf)
        row_max = jnp.max(scores, axis=-1, keepdims=True)
        weights = jnp.exp(scores - row_max)
        weight_sum = jnp.sum(weights, axis=-1)
        rounded = lax.optimization_barrier(weights.astype(jnp.bfloat16)).astype(jnp.float32)
        mixed_sum = jnp.einsum("tkgn,nkd->tkgd", rounded, value_rows)
        return (mixed_sum / weight_sum[..., None]).astype(jnp.bfloat16).reshape(BLOCK, HEADS * HEAD_DIM)

    result = lax.map(one_segment, jnp.arange(N_NODES // 4, dtype=jnp.int32))
    return result.reshape(TOKENS, HEADS * HEAD_DIM)
```

```python
import jax
import jax.numpy as jnp
from jax import lax
from jax.experimental import pallas as pl
from jax.experimental.pallas import tpu as pltpu
from jax.sharding import PartitionSpec as P

HEADS = 16
KV_HEADS = 8
HEAD_DIM = 128
DEPTHS = 4
MEMBERS = 4
GROUP = HEADS // KV_HEADS

query_scale = 168.0 ** (-0.5)
exp2_scale = query_scale * 1.4426950408889634


def dot_t(a, b):
    return lax.dot_general(a, b, (((1,), (1,)), ((), ())), preferred_element_type=jnp.float32)


def dot(a, b):
    return lax.dot_general(a, b, (((1,), (0,)), ((), ())), preferred_element_type=jnp.float32)


def stage_kernel(parent, up, owner, slot, queries, seg_kv, store, *rest):
    send, p0, p1, p2, p3, bias = rest[:6]
    late, (picks, sems) = rest[6:-2], rest[-2:]
    me = lax.axis_index("nodes")
    member = me % MEMBERS
    segment = me // MEMBERS
    segs = parent.shape[0]
    blocks, pages = owner.shape
    q_cols = queries.shape[1] // MEMBERS
    kv_cols = seg_kv.shape[2] // MEMBERS

    def path_rows(g):
        rows = lax.broadcasted_iota(jnp.int32, (blocks, 1), 0)
        current = parent[g]
        on_path = rows == current
        for _ in range(DEPTHS - 1):
            current = jnp.where(current >= 0, up[jnp.maximum(current, 0)], -1)
            on_path = on_path | (rows == current)
        return on_path

    held = owner[...] == me
    pick_of = jnp.max(jnp.where(held, slot[...], 0), axis=1, keepdims=True)

    def one_segment(g, carry):
        pick = jnp.max(jnp.where(path_rows(g), pick_of, 0))
        picks[g] = pick
        for m in range(MEMBERS):
            to = g * MEMBERS + m
            col = m * kv_cols
            pltpu.make_async_copy(
                store.at[0, pick, :, pl.ds(col, HEAD_DIM)], send.at[to, 0], sems.at[4]
            ).start()
            pltpu.make_async_copy(
                store.at[0, pick, :, pl.ds(col + HEAD_DIM, HEAD_DIM)], send.at[to, 1], sems.at[4]
            ).start()
            pltpu.make_async_copy(
                store.at[1, pick, :, pl.ds(col, HEAD_DIM)], send.at[to, 2], sems.at[4]
            ).start()
        return carry

    lax.fori_loop(0, segs, one_segment, 0, unroll=segs <= 4)
    for d, ref in enumerate(late):
        to = me ^ d
        col = pl.multiple_of(to % MEMBERS * kv_cols, kv_cols) + HEAD_DIM
        pltpu.make_async_copy(
            store.at[1, picks[to // MEMBERS], :, pl.ds(pl.multiple_of(col, HEAD_DIM), HEAD_DIM)], ref, sems.at[5 + d]
        ).start()
    for d, piece in enumerate((p0, p1, p2, p3)):
        to = member ^ d
        q_at = pl.multiple_of(to * q_cols, q_cols)
        kv_at = pl.multiple_of(to * kv_cols, kv_cols)
        pltpu.make_async_copy(queries.at[:, pl.ds(q_at, q_cols)], piece.at[:, pl.ds(0, q_cols)], sems.at[d]).start()
        for i in range(2):
            pltpu.make_async_copy(
                seg_kv.at[i, :, pl.ds(kv_at, kv_cols)],
                piece.at[:, pl.ds(q_cols + i * kv_cols, kv_cols)],
                sems.at[d],
            ).start()
    page_tok = store.shape[2]
    mine = path_rows(segment)
    for at in range(0, bias.shape[1], 128):
        page = (lax.broadcasted_iota(jnp.int32, (blocks, 128), 1) + at) // page_tok
        found = jnp.zeros((blocks, 128), jnp.float32)
        for p in range(pages):
            found = jnp.where(mine & (owner[:, p : p + 1] == page), 1.0, found)
        found = jnp.max(found, axis=0, keepdims=True)
        bias[:, at : at + 128] = jnp.where(found > 0.0, 0.0, -jnp.inf)
    for i, ref in enumerate((p0, p1, p2, p3, send, *late)):
        pltpu.make_async_copy(ref, ref, sems.at[i]).wait()


def head_inputs(pieces, h, q_cols, kv_cols):
    q, k, v = [], [], []
    for piece in pieces:
        at = h * GROUP * HEAD_DIM
        q.append([piece[:, at + i * HEAD_DIM : at + (i + 1) * HEAD_DIM] for i in range(GROUP)])
        at = q_cols + h * HEAD_DIM
        k.append(piece[:, at : at + HEAD_DIM])
        v.append(piece[:, at + kv_cols : at + kv_cols + HEAD_DIM])
    queries = [jnp.concatenate(one, axis=0) for one in q]
    return queries, jnp.concatenate(k, axis=0), jnp.concatenate(v, axis=0)


def own_mask(member, d, rows, tok):
    cols = MEMBERS * tok
    r = lax.broadcasted_iota(jnp.int32, (rows, cols), 0)
    c = lax.broadcasted_iota(jnp.int32, (rows, cols), 1)
    q_at = (member ^ d) * tok + r % tok
    k_at = (member ^ (c // tok)) * tok + c % tok
    return k_at <= q_at


def softmax_parts(q, k_own, k_pages, bias_ref, score_ref, visible, step):
    keys = k_pages.shape[0]
    own = jnp.where(visible, dot_t(q, k_own), -jnp.inf)
    top = jnp.max(own, axis=1, keepdims=True)
    for at in range(0, keys, step):
        s = dot_t(q, k_pages[at : at + step]) + bias_ref[:, at : at + step]
        score_ref[:, at : at + step] = s
        top = jnp.maximum(top, jnp.max(s, axis=1, keepdims=True))
    top = top * exp2_scale
    own = jnp.exp2(own * exp2_scale - top)
    return own, top


def full_kernel(page_tok, h, bias_ref, p0, p1, p2, p3, pages, o0, o1, o2, o3, score_ref):
    member = lax.axis_index("nodes") % MEMBERS
    tok = p0.shape[0]
    q_cols = p0.shape[1] // 2
    kv_cols = q_cols // GROUP
    queries, k_own, v_own = head_inputs((p0, p1, p2, p3), h, q_cols, kv_cols)
    keys = pages.shape[0] * page_tok
    step = min(keys, 512)
    k_pages = pages[:, 0].reshape(keys, HEAD_DIM)
    for d, out in enumerate((o0, o1, o2, o3)):
        visible = own_mask(member, d, GROUP * tok, tok)
        own, top = softmax_parts(queries[d], k_own, k_pages, bias_ref, score_ref, visible, step)
        total = jnp.sum(own, axis=1, keepdims=True)
        mixed = dot(own.astype(jnp.bfloat16), v_own)
        for at in range(0, keys, step):
            w = jnp.exp2(score_ref[:, at : at + step] * exp2_scale - top)
            total = total + jnp.sum(w, axis=1, keepdims=True)
            v = pages[at // page_tok : (at + step) // page_tok, 2].reshape(step, HEAD_DIM)
            mixed = mixed + dot(w.astype(jnp.bfloat16), v)
        res = (mixed / total).astype(jnp.bfloat16)
        for i in range(GROUP):
            out[:, i * HEAD_DIM : (i + 1) * HEAD_DIM] = res[i * tok : (i + 1) * tok]


def weights_kernel(page_tok, h, bias_ref, p0, p1, p2, p3, pages, w_ref, mixed_ref, total_ref, score_ref):
    member = lax.axis_index("nodes") % MEMBERS
    tok = p0.shape[0]
    q_cols = p0.shape[1] // 2
    kv_cols = q_cols // GROUP
    queries, k_own, v_own = head_inputs((p0, p1, p2, p3), h, q_cols, kv_cols)
    keys = pages.shape[0] * page_tok
    step = min(keys, 512)
    k_pages = pages[:, 1].reshape(keys, HEAD_DIM)
    for d in range(MEMBERS):
        visible = own_mask(member, d, GROUP * tok, tok)
        own, top = softmax_parts(queries[d], k_own, k_pages, bias_ref, score_ref, visible, step)
        total = jnp.sum(own, axis=1, keepdims=True)
        mixed_ref[d] = dot(own.astype(jnp.bfloat16), v_own)
        for at in range(0, keys, step):
            w = jnp.exp2(score_ref[:, at : at + step] * exp2_scale - top)
            total = total + jnp.sum(w, axis=1, keepdims=True)
            w_ref[d, :, at : at + step] = w.astype(jnp.bfloat16)
        total_ref[d] = jnp.broadcast_to(total, total_ref.shape[1:])


def values_kernel(w_ref, mixed_ref, total_ref, *rest):
    late, outs, v_ref = rest[: -MEMBERS - 1], rest[-MEMBERS - 1 : -1], rest[-1]
    me = lax.axis_index("nodes")
    tok = outs[0].shape[0]
    page_tok = late[0].shape[0]
    for d, ref in enumerate(late):
        v_ref[pl.ds(pl.multiple_of((me ^ d) * page_tok, page_tok), page_tok)] = ref[...]
    for d, out in enumerate(outs):
        mixed = mixed_ref[d] + dot(w_ref[d], v_ref[...])
        res = (mixed / total_ref[d]).astype(jnp.bfloat16)
        for i in range(GROUP):
            out[:, i * HEAD_DIM : (i + 1) * HEAD_DIM] = res[i * tok : (i + 1) * tok]


def join_kernel(*refs):
    parts, out, sems = refs[:8], refs[8], refs[9]
    member = lax.axis_index("nodes") % MEMBERS
    width = parts[0].shape[1]
    copies = []
    for h in range(2):
        for d in range(MEMBERS):
            at = pl.multiple_of(((member ^ d) * 2 + h) * width, width)
            i = h * MEMBERS + d
            copies.append(pltpu.make_async_copy(parts[i], out.at[:, pl.ds(at, width)], sems.at[i]))
    for c in copies:
        c.start()
    for c in copies:
        c.wait()


def local(queries, seg_kv, kv_store, seg_parent, block_up, page_owner, page_slot):
    nodes = lax.axis_size("nodes")
    tok = queries.shape[0]
    page_tok = kv_store.shape[2]
    keys = nodes * page_tok
    bf16, f32 = jnp.bfloat16, jnp.float32
    any_spec = pl.BlockSpec(memory_space=pl.ANY)
    smem = pl.BlockSpec(memory_space=pltpu.SMEM)
    vmem = pl.BlockSpec(memory_space=pltpu.VMEM)
    params = pltpu.CompilerParams(vmem_limit_bytes=24 * 2**20)
    piece = jax.ShapeDtypeStruct((tok, queries.shape[1] // MEMBERS + 2 * seg_kv.shape[2] // MEMBERS), bf16)
    late = jax.ShapeDtypeStruct((page_tok, HEAD_DIM), bf16)
    early = jax.ShapeDtypeStruct((nodes, 3, page_tok, HEAD_DIM), bf16)
    staged = pl.pallas_call(
        stage_kernel,
        in_specs=[smem] * 2 + [vmem] * 2 + [any_spec] * 3,
        out_specs=[vmem] * (6 + nodes),
        out_shape=[early, *[piece] * MEMBERS, jax.ShapeDtypeStruct((1, keys), f32), *[late] * nodes],
        scratch_shapes=[pltpu.SMEM((nodes // MEMBERS,), jnp.int32), pltpu.SemaphoreType.DMA((5 + nodes,))],
        compiler_params=params,
        name="stage",
    )(seg_parent, block_up, page_owner, page_slot, queries, seg_kv, kv_store)
    send, p0, p1, p2, p3, bias = staged[:6]
    held = staged[6:]

    def exchange(x):
        return lax.all_to_all(x, "nodes", split_axis=0, concat_axis=0, tiled=True)

    def swapped(x, d):
        return lax.ppermute(x, "nodes", [(i, i ^ d) for i in range(nodes)])

    got = exchange(send)
    pieces = (p0, swapped(p1, 1), swapped(p2, 2), swapped(p3, 3))
    values = [held[0]] + [swapped(held[d], d) for d in range(1, nodes)]
    rows = GROUP * tok
    scratch = [pltpu.VMEM((rows, keys), f32)]
    out_piece = jax.ShapeDtypeStruct((tok, GROUP * HEAD_DIM), bf16)
    out_a = pl.pallas_call(
        lambda *refs: full_kernel(page_tok, 0, *refs),
        in_specs=[vmem] * 6,
        out_specs=[vmem] * 4,
        out_shape=[out_piece] * 4,
        scratch_shapes=scratch,
        compiler_params=params,
        name="full",
    )(bias, *pieces, got)
    weights, mixed, total = pl.pallas_call(
        lambda *refs: weights_kernel(page_tok, 1, *refs),
        in_specs=[vmem] * 6,
        out_specs=[vmem] * 3,
        out_shape=[
            jax.ShapeDtypeStruct((MEMBERS, rows, keys), bf16),
            jax.ShapeDtypeStruct((MEMBERS, rows, HEAD_DIM), f32),
            jax.ShapeDtypeStruct((MEMBERS, rows, HEAD_DIM), f32),
        ],
        scratch_shapes=scratch,
        compiler_params=params,
        name="weights",
    )(bias, *pieces, got)
    out_b = pl.pallas_call(
        values_kernel,
        in_specs=[vmem] * (3 + nodes),
        out_specs=[vmem] * 4,
        out_shape=[out_piece] * 4,
        scratch_shapes=[pltpu.VMEM((keys, HEAD_DIM), bf16)],
        compiler_params=params,
        name="values",
    )(weights, mixed, total, *values)
    parts = []
    for one in (out_a, out_b):
        parts += [one[0]] + [swapped(one[d], d) for d in range(1, MEMBERS)]
    return pl.pallas_call(
        join_kernel,
        in_specs=[vmem] * 8,
        out_specs=any_spec,
        out_shape=jax.ShapeDtypeStruct(queries.shape, bf16),
        scratch_shapes=[pltpu.SemaphoreType.DMA((8,))],
        compiler_params=params,
        name="join",
    )(*parts)


def solution(mesh):
    in_specs = (
        P(("groups", "nodes"), None),
        P(None, ("groups", "nodes"), None),
        P(None, ("groups", "nodes"), None, None),
        P("groups"),
        P("groups"),
        P("groups", None),
        P("groups", None),
    )
    out_specs = P(("groups", "nodes"), None)

    return jax.shard_map(local, mesh=mesh, in_specs=in_specs, out_specs=out_specs, check_vma=False)
```

```python
import jax
import jax.numpy as jnp
from jax import lax
from jax.experimental import pallas as pl
from jax.experimental.pallas import tpu as pltpu
from jax.sharding import PartitionSpec as P


HEADS = 16
KV_HEADS = 8
HEAD_DIM = 128
DEPTHS = 4
MEMBERS = 4
STAGE_VMEM = 60 * 1024 * 2**10
PIECES_VMEM = 52 * 2**20
GROUP = HEADS // KV_HEADS

query_scale = 168.0 ** (-0.5)
exp2_scale = query_scale * 1.4426950408889634


def dot_t(a, b):
    return lax.dot_general(a, b, (((1,), (1,)), ((), ())), preferred_element_type=jnp.float32)


def dot(a, b):
    return lax.dot_general(a, b, (((1,), (0,)), ((), ())), preferred_element_type=jnp.float32)


def walk(parent, up, g):
    out = [parent[g]]
    for _ in range(DEPTHS - 1):
        out.append(jnp.where(out[-1] >= 0, up[jnp.maximum(out[-1], 0)], -1))
    return out


def stage_kernel(parent_in, up_in, owner_in, slot_in, store, send, picks, parent, up, owner, slot, sems):
    tables = ((parent_in, parent), (up_in, up), (owner_in, owner), (slot_in, slot))
    copies = [pltpu.make_async_copy(src, dst, sems.at[i]) for i, (src, dst) in enumerate(tables)]
    for c in copies:
        c.start()
    me = lax.axis_index("nodes")
    segs = parent.shape[0]
    _, blocks = owner.shape
    kv_cols = store.shape[3] // MEMBERS
    sem = sems.at[len(copies)]
    for c in copies:
        c.wait()
    pick_of = jnp.max(jnp.where(owner[...] == me, slot[...], 0), axis=0, keepdims=True)
    lanes = lax.broadcasted_iota(jnp.int32, (1, blocks), 1)

    def one_segment(g, carry):
        on_path = lanes < 0
        for block in walk(parent, up, g):
            on_path = on_path | (lanes == block)
        pick = jnp.max(jnp.where(on_path, pick_of, 0))
        picks[g] = pick
        for m in range(MEMBERS):
            to = g * MEMBERS + m
            col = m * kv_cols
            for i, (kind, at) in enumerate(((0, col), (0, col + HEAD_DIM), (1, col))):
                pltpu.make_async_copy(store.at[kind, pick, :, pl.ds(at, HEAD_DIM)], send.at[to, i], sem).start()
        return carry

    lax.fori_loop(0, segs, one_segment, 0, unroll=segs <= 4)
    pltpu.make_async_copy(send, send, sem).wait()


def late_place(g, tok, page_tok):
    stack = tok // page_tok
    return g % stack * page_tok, g // stack


def pieces_kernel(parent, up, owner, picks, queries, seg_kv, store, p0, p1, p2, p3, bias, sems):
    member = lax.axis_index("nodes") % MEMBERS
    tok = queries.shape[0]
    page_tok = store.shape[2]
    q_cols = queries.shape[1] // MEMBERS
    kv_cols = seg_kv.shape[2] // MEMBERS
    own_cols = q_cols + 2 * kv_cols
    for d, piece in enumerate((p0, p1, p2, p3)):
        to = member ^ d
        q_at = pl.multiple_of(to * q_cols, q_cols)
        kv_at = pl.multiple_of(to * kv_cols, kv_cols)
        pltpu.make_async_copy(queries.at[:, pl.ds(q_at, q_cols)], piece.at[:, pl.ds(0, q_cols)], sems.at[d]).start()
        for i in range(2):
            pltpu.make_async_copy(
                seg_kv.at[i, :, pl.ds(kv_at, kv_cols)],
                piece.at[:, pl.ds(q_cols + i * kv_cols, kv_cols)],
                sems.at[d],
            ).start()
        col = pl.multiple_of(to * kv_cols + HEAD_DIM, HEAD_DIM)
        for g in range(parent.shape[0]):
            row, block = late_place(g, tok, page_tok)
            pltpu.make_async_copy(
                store.at[1, picks[g], :, pl.ds(col, HEAD_DIM)],
                piece.at[pl.ds(row, page_tok), pl.ds(own_cols + block * HEAD_DIM, HEAD_DIM)],
                sems.at[d],
            ).start()
    page_bias(parent, up, owner, bias, page_tok)
    for i, ref in enumerate((p0, p1, p2, p3)):
        pltpu.make_async_copy(ref, ref, sems.at[i]).wait()


def relay_kernel(p0, p1, p2, p3, *rest):
    outs, sems = rest[:-1], rest[-1]
    me = lax.axis_index("nodes")
    member, segment = me % MEMBERS, me // MEMBERS
    tok, cols = p0.shape
    page_tok = outs[0].shape[1]
    late_cols = len(outs) * page_tok * HEAD_DIM // tok
    for e, out in enumerate(outs):
        row, block = late_place(segment ^ e, tok, page_tok)
        col = pl.multiple_of(cols - late_cols + block * HEAD_DIM, HEAD_DIM)
        row = pl.multiple_of(row, page_tok)
        for d, piece in enumerate((p0, p1, p2, p3)):
            pltpu.make_async_copy(
                piece.at[pl.ds(row, page_tok), pl.ds(col, HEAD_DIM)], out.at[member ^ d], sems.at[e]
            ).start()
    for e, out in enumerate(outs):
        pltpu.make_async_copy(out, out, sems.at[e]).wait()


def page_bias(parent, up, owner, bias_ref, page_tok):
    pages, blocks = owner.shape
    path = walk(parent, up, lax.axis_index("nodes") // MEMBERS)
    rows = lax.broadcasted_iota(jnp.int32, (8, blocks), 0)
    block_at = jnp.full((8, blocks), -1, jnp.int32)
    for i, block in enumerate(path):
        block_at = jnp.where(rows == i, block, block_at)
    chosen = (lax.broadcasted_iota(jnp.int32, (8, blocks), 1) == block_at).astype(jnp.float32)
    above = owner[...].astype(jnp.float32) + 1.0
    held_by = lax.dot_general(
        chosen, above, (((1,), (1,)), ((), ())), precision=lax.Precision.HIGHEST, preferred_element_type=jnp.float32
    )
    held_by = (held_by + 0.5).astype(jnp.int32) - 1
    for at in range(0, bias_ref.shape[1], 128):
        page = (lax.broadcasted_iota(jnp.int32, (8, 128), 1) + at) // page_tok
        found = jnp.zeros((8, 128), jnp.float32)
        for p in range(pages):
            found = jnp.where(held_by[:, p : p + 1] == page, 1.0, found)
        found = jnp.max(found, axis=0, keepdims=True)
        bias_ref[:, at : at + 128] = jnp.where(found > 0.0, 0.0, -jnp.inf)


def head_inputs(pieces, h, q_cols, kv_cols):
    q, k, v = [], [], []
    for piece in pieces:
        at = h * GROUP * HEAD_DIM
        q.append([piece[:, at + i * HEAD_DIM : at + (i + 1) * HEAD_DIM] for i in range(GROUP)])
        at = q_cols + h * HEAD_DIM
        k.append(piece[:, at : at + HEAD_DIM])
        v.append(piece[:, at + kv_cols : at + kv_cols + HEAD_DIM])
    queries = [jnp.concatenate(one, axis=0) for one in q]
    return queries, jnp.concatenate(k, axis=0), jnp.concatenate(v, axis=0)


def own_mask(member, d, rows, tok):
    cols = MEMBERS * tok
    r = lax.broadcasted_iota(jnp.int32, (rows, cols), 0)
    c = lax.broadcasted_iota(jnp.int32, (rows, cols), 1)
    q_at = (member ^ d) * tok + r % tok
    k_at = (member ^ (c // tok)) * tok + c % tok
    return k_at <= q_at


def softmax_parts(q, k_own, k_pages, bias_ref, score_ref, visible, step):
    keys = k_pages.shape[0]
    own = jnp.where(visible, dot_t(q, k_own), -jnp.inf)
    top = jnp.max(own, axis=1, keepdims=True)
    for at in range(0, keys, step):
        s = dot_t(q, k_pages[at : at + step]) + bias_ref[:, at : at + step]
        score_ref[:, at : at + step] = s
        top = jnp.maximum(top, jnp.max(s, axis=1, keepdims=True))
    top = top * exp2_scale
    own = jnp.exp2(own * exp2_scale - top)
    return own, top


def full_kernel(page_tok, h, bias_ref, p0, p1, p2, p3, pages, o0, o1, o2, o3, score_ref):
    member = lax.axis_index("nodes") % MEMBERS
    tok = p0.shape[0]
    q_cols = HEADS // MEMBERS * HEAD_DIM
    kv_cols = q_cols // GROUP
    queries, k_own, v_own = head_inputs((p0, p1, p2, p3), h, q_cols, kv_cols)
    keys = pages.shape[0] * page_tok
    step = min(keys, 512)
    k_pages = pages[:, 0].reshape(keys, HEAD_DIM)
    for d, out in enumerate((o0, o1, o2, o3)):
        visible = own_mask(member, d, GROUP * tok, tok)
        own, top = softmax_parts(queries[d], k_own, k_pages, bias_ref, score_ref, visible, step)
        total = jnp.sum(own, axis=1, keepdims=True)
        mixed = dot(own.astype(jnp.bfloat16), v_own)
        for at in range(0, keys, step):
            w = jnp.exp2(score_ref[:, at : at + step] * exp2_scale - top)
            total = total + jnp.sum(w, axis=1, keepdims=True)
            v = pages[at // page_tok : (at + step) // page_tok, 2].reshape(step, HEAD_DIM)
            mixed = mixed + dot(w.astype(jnp.bfloat16), v)
        res = (mixed / total).astype(jnp.bfloat16)
        for i in range(GROUP):
            out[:, i * HEAD_DIM : (i + 1) * HEAD_DIM] = res[i * tok : (i + 1) * tok]


def weights_kernel(page_tok, h, bias_ref, p0, p1, p2, p3, pages, w_ref, mixed_ref, total_ref, score_ref):
    member = lax.axis_index("nodes") % MEMBERS
    tok = p0.shape[0]
    q_cols = HEADS // MEMBERS * HEAD_DIM
    kv_cols = q_cols // GROUP
    queries, k_own, v_own = head_inputs((p0, p1, p2, p3), h, q_cols, kv_cols)
    keys = pages.shape[0] * page_tok
    step = min(keys, 512)
    k_pages = pages[:, 1].reshape(keys, HEAD_DIM)
    for d in range(MEMBERS):
        visible = own_mask(member, d, GROUP * tok, tok)
        own, top = softmax_parts(queries[d], k_own, k_pages, bias_ref, score_ref, visible, step)
        total = jnp.sum(own, axis=1, keepdims=True)
        mixed_ref[d] = dot(own.astype(jnp.bfloat16), v_own)
        for at in range(0, keys, step):
            w = jnp.exp2(score_ref[:, at : at + step] * exp2_scale - top)
            total = total + jnp.sum(w, axis=1, keepdims=True)
            w_ref[d, :, at : at + step] = w.astype(jnp.bfloat16)
        total_ref[d] = jnp.broadcast_to(total, total_ref.shape[1:])


def values_kernel(w_ref, mixed_ref, total_ref, *rest):
    late, outs, v_ref = rest[: -MEMBERS - 1], rest[-MEMBERS - 1 : -1], rest[-1]
    me = lax.axis_index("nodes")
    tok = outs[0].shape[0]
    rows = MEMBERS * late[0].shape[1]
    for e, ref in enumerate(late):
        at = pl.multiple_of((me // MEMBERS ^ e) * rows, rows)
        v_ref[pl.ds(at, rows)] = ref[...].reshape(rows, HEAD_DIM)
    for d, out in enumerate(outs):
        mixed = mixed_ref[d] + dot(w_ref[d], v_ref[...])
        res = (mixed / total_ref[d]).astype(jnp.bfloat16)
        for i in range(GROUP):
            out[:, i * HEAD_DIM : (i + 1) * HEAD_DIM] = res[i * tok : (i + 1) * tok]


def join_kernel(*refs):
    parts, out, sems = refs[:8], refs[8], refs[9]
    member = lax.axis_index("nodes") % MEMBERS
    width = parts[0].shape[1]
    copies = []
    for h in range(2):
        for d in range(MEMBERS):
            at = pl.multiple_of(((member ^ d) * 2 + h) * width, width)
            i = h * MEMBERS + d
            copies.append(pltpu.make_async_copy(parts[i], out.at[:, pl.ds(at, width)], sems.at[i]))
    for c in copies:
        c.start()
    for c in copies:
        c.wait()


def local(queries, seg_kv, kv_store, seg_parent, block_up, page_owner, page_slot):
    nodes = lax.axis_size("nodes")
    segs = nodes // MEMBERS
    tok = queries.shape[0]
    page_tok = kv_store.shape[2]
    keys = nodes * page_tok
    bf16, f32, i32 = jnp.bfloat16, jnp.float32, jnp.int32
    hbm = pl.BlockSpec(memory_space=pltpu.HBM)
    smem = pl.BlockSpec(memory_space=pltpu.SMEM)
    vmem = pl.BlockSpec(memory_space=pltpu.VMEM)
    params = pltpu.CompilerParams(vmem_limit_bytes=24 * 2**20)
    wide = pltpu.CompilerParams(vmem_limit_bytes=STAGE_VMEM)
    late_cols = segs * page_tok * HEAD_DIM // tok
    piece_cols = (queries.shape[1] + 2 * seg_kv.shape[2]) // MEMBERS + late_cols
    piece = jax.ShapeDtypeStruct((tok, piece_cols), bf16)
    late = jax.ShapeDtypeStruct((MEMBERS, page_tok, HEAD_DIM), bf16)
    early = jax.ShapeDtypeStruct((nodes, 3, page_tok, HEAD_DIM), bf16)
    owner_of, slot_of = page_owner.T, page_slot.T
    send, picks = pl.pallas_call(
        stage_kernel,
        in_specs=[hbm] * 5,
        out_specs=[vmem, smem],
        out_shape=[early, jax.ShapeDtypeStruct((segs,), i32)],
        scratch_shapes=[
            pltpu.SMEM(seg_parent.shape, i32),
            pltpu.SMEM(block_up.shape, i32),
            pltpu.VMEM(owner_of.shape, i32),
            pltpu.VMEM(slot_of.shape, i32),
            pltpu.SemaphoreType.DMA((5,)),
        ],
        compiler_params=wide,
        name="stage",
    )(seg_parent, block_up, owner_of, slot_of, kv_store)
    *sends, bias = pl.pallas_call(
        pieces_kernel,
        in_specs=[smem] * 2 + [vmem] + [smem] + [hbm] * 3,
        out_specs=[vmem] * (MEMBERS + 1),
        out_shape=[piece] * MEMBERS + [jax.ShapeDtypeStruct((1, keys), f32)],
        scratch_shapes=[pltpu.SemaphoreType.DMA((MEMBERS,))],
        compiler_params=pltpu.CompilerParams(vmem_limit_bytes=PIECES_VMEM),
        name="pieces",
    )(seg_parent, block_up, owner_of, picks, queries, seg_kv, kv_store)

    def swapped(x, d):
        return lax.ppermute(x, "nodes", [(i, i ^ d) for i in range(nodes)])

    got = lax.all_to_all(send, "nodes", split_axis=0, concat_axis=0, tiled=True)
    pieces = [sends[0]] + [swapped(sends[d], d) for d in range(1, MEMBERS)]
    held = pl.pallas_call(
        relay_kernel,
        in_specs=[vmem] * MEMBERS,
        out_specs=[vmem] * segs,
        out_shape=[late] * segs,
        scratch_shapes=[pltpu.SemaphoreType.DMA((segs,))],
        compiler_params=params,
        name="relay",
    )(*pieces)
    values = [held[0]] + [swapped(held[e], e * MEMBERS) for e in range(1, segs)]
    rows = GROUP * tok
    scratch = [pltpu.VMEM((rows, keys), f32)]
    out_piece = jax.ShapeDtypeStruct((tok, GROUP * HEAD_DIM), bf16)
    out_a = pl.pallas_call(
        lambda *refs: full_kernel(page_tok, 0, *refs),
        in_specs=[vmem] * 6,
        out_specs=[vmem] * 4,
        out_shape=[out_piece] * 4,
        scratch_shapes=scratch,
        compiler_params=params,
        name="full",
    )(bias, *pieces, got)
    weights, mixed, total = pl.pallas_call(
        lambda *refs: weights_kernel(page_tok, 1, *refs),
        in_specs=[vmem] * 6,
        out_specs=[vmem] * 3,
        out_shape=[
            jax.ShapeDtypeStruct((MEMBERS, rows, keys), bf16),
            jax.ShapeDtypeStruct((MEMBERS, rows, HEAD_DIM), f32),
            jax.ShapeDtypeStruct((MEMBERS, rows, HEAD_DIM), f32),
        ],
        scratch_shapes=scratch,
        compiler_params=params,
        name="weights",
    )(bias, *pieces, got)
    out_b = pl.pallas_call(
        values_kernel,
        in_specs=[vmem] * (3 + segs),
        out_specs=[vmem] * 4,
        out_shape=[out_piece] * 4,
        scratch_shapes=[pltpu.VMEM((keys, HEAD_DIM), bf16)],
        compiler_params=params,
        name="values",
    )(weights, mixed, total, *values)
    parts = []
    for one in (out_a, out_b):
        parts += [one[0]] + [swapped(one[d], d) for d in range(1, MEMBERS)]
    return pl.pallas_call(
        join_kernel,
        in_specs=[vmem] * 8,
        out_specs=hbm,
        out_shape=jax.ShapeDtypeStruct(queries.shape, bf16),
        scratch_shapes=[pltpu.SemaphoreType.DMA((8,))],
        compiler_params=params,
        name="join",
    )(*parts)


def solution(mesh):
    in_specs = (
        P(("groups", "nodes"), None),
        P(None, ("groups", "nodes"), None),
        P(None, ("groups", "nodes"), None, None),
        P("groups"),
        P("groups"),
        P("groups", None),
        P("groups", None),
    )
    out_specs = P(("groups", "nodes"), None)

    return jax.shard_map(local, mesh=mesh, in_specs=in_specs, out_specs=out_specs, check_vma=False)
```

```python
import jax
import jax.numpy as jnp
from jax import lax
from jax.experimental import pallas as pl
from jax.experimental.pallas import tpu as pltpu
from jax.sharding import PartitionSpec as P


HEADS = 16
KV_HEADS = 8
HEAD_DIM = 128
DEPTHS = 4
MEMBERS = 4
GROUP = HEADS // KV_HEADS
KV_COLS = KV_HEADS // MEMBERS * HEAD_DIM
OWN_COLS = HEADS // MEMBERS * HEAD_DIM + 2 * KV_COLS
STAGE_VMEM = 60 * 1024 * 2**10
PIECES_VMEM = 52 * 2**20

query_scale = 168.0 ** (-0.5)
exp2_scale = query_scale * 1.4426950408889634


def dot_t(a, b):
    return lax.dot_general(a, b, (((1,), (1,)), ((), ())), preferred_element_type=jnp.float32)


def dot(a, b):
    return lax.dot_general(a, b, (((1,), (0,)), ((), ())), preferred_element_type=jnp.float32)


def walk(parent, up, g):
    out = [parent[g]]
    for _ in range(DEPTHS - 1):
        out.append(jnp.where(out[-1] >= 0, up[jnp.maximum(out[-1], 0)], -1))
    return out


HEADS_HERE = KV_HEADS // MEMBERS


def stage_kernel(parent_in, up_in, owner_in, slot_in, store, send, picks, parent, up, owner, slot, sems):
    tables = ((parent_in, parent), (up_in, up), (owner_in, owner), (slot_in, slot))
    copies = [pltpu.make_async_copy(src, dst, sems.at[i]) for i, (src, dst) in enumerate(tables)]
    for c in copies:
        c.start()
    me = lax.axis_index("nodes")
    segs = parent.shape[0]
    blocks = owner.shape[1]
    sem = sems.at[len(copies)]
    for c in copies:
        c.wait()
    pick_of = jnp.max(jnp.where(owner[...] == me, slot[...], 0), axis=0, keepdims=True)
    lanes = lax.broadcasted_iota(jnp.int32, (1, blocks), 1)

    def one_segment(g, carry):
        on_path = lanes < 0
        for block in walk(parent, up, g):
            on_path = on_path | (lanes == block)
        pick = jnp.max(jnp.where(on_path, pick_of, 0))
        picks[g] = pick
        for m in range(MEMBERS):
            src = store.at[0, pick, :, pl.ds(m * KV_COLS, KV_COLS)]
            pltpu.make_async_copy(src, send.at[g * MEMBERS + m], sem).start()
        return carry

    lax.fori_loop(0, segs, one_segment, 0, unroll=segs <= 4)
    pltpu.make_async_copy(send, send, sem).wait()


def pieces_kernel(parent, up, owner, picks, queries, seg_kv, store, bias, *rest):
    owns, late, sems = rest[:MEMBERS], rest[MEMBERS:-1], rest[-1]
    me = lax.axis_index("nodes")
    member = me % MEMBERS
    page_tok = store.shape[2]
    q_cols = queries.shape[1] // MEMBERS
    kv_cols = seg_kv.shape[2] // MEMBERS
    for d in range(MEMBERS):
        to = member ^ d
        q_at = pl.multiple_of(to * q_cols, q_cols)
        kv_at = pl.multiple_of(to * kv_cols, kv_cols)
        sem = sems.at[d]
        pltpu.make_async_copy(queries.at[:, pl.ds(q_at, q_cols)], owns[d].at[:, pl.ds(0, q_cols)], sem).start()
        for i in range(2):
            pltpu.make_async_copy(
                seg_kv.at[i, :, pl.ds(kv_at, kv_cols)], owns[d].at[:, pl.ds(q_cols + i * kv_cols, kv_cols)], sem
            ).start()
    for d, ref in enumerate(late):
        to = me ^ d
        at = pl.multiple_of(to % MEMBERS * KV_COLS, KV_COLS)
        pltpu.make_async_copy(
            store.at[1, picks[to // MEMBERS], :, pl.ds(at, KV_COLS)], ref, sems.at[MEMBERS + d]
        ).start()
    page_bias(parent, up, owner, bias, page_tok)
    for i, ref in enumerate((*owns, *late)):
        pltpu.make_async_copy(ref, ref, sems.at[i]).wait()


def page_bias(parent, up, owner, bias_ref, page_tok):
    pages, blocks = owner.shape
    path = walk(parent, up, lax.axis_index("nodes") // MEMBERS)
    rows = lax.broadcasted_iota(jnp.int32, (8, blocks), 0)
    block_at = jnp.full((8, blocks), -1, jnp.int32)
    for i, block in enumerate(path):
        block_at = jnp.where(rows == i, block, block_at)
    chosen = (lax.broadcasted_iota(jnp.int32, (8, blocks), 1) == block_at).astype(jnp.float32)
    above = owner[...].astype(jnp.float32) + 1.0
    held_by = lax.dot_general(
        chosen, above, (((1,), (1,)), ((), ())), precision=lax.Precision.HIGHEST, preferred_element_type=jnp.float32
    )
    held_by = (held_by + 0.5).astype(jnp.int32) - 1
    for at in range(0, bias_ref.shape[1], 128):
        page = (lax.broadcasted_iota(jnp.int32, (8, 128), 1) + at) // page_tok
        found = jnp.zeros((8, 128), jnp.float32)
        for p in range(pages):
            found = jnp.where(held_by[:, p : p + 1] == page, 1.0, found)
        found = jnp.max(found, axis=0, keepdims=True)
        bias_ref[:, at : at + 128] = jnp.where(found > 0.0, 0.0, -jnp.inf)


def head_inputs(pieces, h):
    q_cols, kv_cols = GROUP * KV_COLS, KV_COLS
    q, k, v = [], [], []
    for piece in pieces:
        at = h * GROUP * HEAD_DIM
        q.append([piece[:, at + i * HEAD_DIM : at + (i + 1) * HEAD_DIM] for i in range(GROUP)])
        at = q_cols + h * HEAD_DIM
        k.append(piece[:, at : at + HEAD_DIM])
        v.append(piece[:, at + kv_cols : at + kv_cols + HEAD_DIM])
    queries = [jnp.concatenate(one, axis=0) for one in q]
    return queries, jnp.concatenate(k, axis=0), jnp.concatenate(v, axis=0)


def own_mask(member, d, rows, tok):
    cols = MEMBERS * tok
    r = lax.broadcasted_iota(jnp.int32, (rows, cols), 0)
    c = lax.broadcasted_iota(jnp.int32, (rows, cols), 1)
    q_at = (member ^ d) * tok + r % tok
    k_at = (member ^ (c // tok)) * tok + c % tok
    return k_at <= q_at


def softmax_parts(q, k_own, k_pages, bias_ref, score_ref, visible, step):
    keys = k_pages.shape[0]
    own = jnp.where(visible, dot_t(q, k_own), -jnp.inf)
    top = jnp.max(own, axis=1, keepdims=True)
    for at in range(0, keys, step):
        s = dot_t(q, k_pages[at : at + step]) + bias_ref[:, at : at + step]
        score_ref[:, at : at + step] = s
        top = jnp.maximum(top, jnp.max(s, axis=1, keepdims=True))
    top = top * exp2_scale
    own = jnp.exp2(own * exp2_scale - top)
    return own, top


def weights_kernel(bias_ref, p0, p1, p2, p3, pages, *rest):
    results, score_ref = rest[:-1], rest[-1]
    member = lax.axis_index("nodes") % MEMBERS
    tok = p0.shape[0]
    keys = bias_ref.shape[1]
    step = min(keys, 512)
    for h in range(HEADS_HERE):
        w_ref, mixed_ref, total_ref = results[3 * h : 3 * h + 3]
        queries, k_own, v_own = head_inputs((p0, p1, p2, p3), h)
        k_pages = pages[:, :, h * HEAD_DIM : (h + 1) * HEAD_DIM].reshape(keys, HEAD_DIM)
        for d in range(MEMBERS):
            visible = own_mask(member, d, GROUP * tok, tok)
            own, top = softmax_parts(queries[d], k_own, k_pages, bias_ref, score_ref, visible, step)
            total = jnp.sum(own, axis=1, keepdims=True)
            mixed_ref[d] = dot(own.astype(jnp.bfloat16), v_own)
            for at in range(0, keys, step):
                w = jnp.exp2(score_ref[:, at : at + step] * exp2_scale - top)
                total = total + jnp.sum(w, axis=1, keepdims=True)
                w_ref[d, :, at : at + step] = w.astype(jnp.bfloat16)
            total_ref[d] = jnp.broadcast_to(total, total_ref.shape[1:])


def values_kernel(h, w_ref, mixed_ref, total_ref, *rest):
    late, outs, v_ref = rest[: -MEMBERS - 1], rest[-MEMBERS - 1 : -1], rest[-1]
    me = lax.axis_index("nodes")
    tok = outs[0].shape[0]
    rows = late[0].shape[0]
    for d, ref in enumerate(late):
        v_ref[pl.ds(pl.multiple_of((me ^ d) * rows, rows), rows)] = ref[:, h * HEAD_DIM : (h + 1) * HEAD_DIM]
    for d, out in enumerate(outs):
        mixed = mixed_ref[d] + dot(w_ref[d], v_ref[...])
        res = (mixed / total_ref[d]).astype(jnp.bfloat16)
        for i in range(GROUP):
            out[:, i * HEAD_DIM : (i + 1) * HEAD_DIM] = res[i * tok : (i + 1) * tok]


def join_kernel(*refs):
    parts, out, sems = refs[:8], refs[8], refs[9]
    member = lax.axis_index("nodes") % MEMBERS
    width = parts[0].shape[1]
    copies = []
    for h in range(2):
        for d in range(MEMBERS):
            at = pl.multiple_of(((member ^ d) * 2 + h) * width, width)
            i = h * MEMBERS + d
            copies.append(pltpu.make_async_copy(parts[i], out.at[:, pl.ds(at, width)], sems.at[i]))
    for c in copies:
        c.start()
    for c in copies:
        c.wait()


def local(queries, seg_kv, kv_store, seg_parent, block_up, page_owner, page_slot):
    nodes = lax.axis_size("nodes")
    segs = nodes // MEMBERS
    tok = queries.shape[0]
    page_tok = kv_store.shape[2]
    keys = nodes * page_tok
    bf16, f32, i32 = jnp.bfloat16, jnp.float32, jnp.int32
    hbm = pl.BlockSpec(memory_space=pltpu.HBM)
    smem = pl.BlockSpec(memory_space=pltpu.SMEM)
    vmem = pl.BlockSpec(memory_space=pltpu.VMEM)
    params = pltpu.CompilerParams(vmem_limit_bytes=24 * 2**20)
    wide = pltpu.CompilerParams(vmem_limit_bytes=STAGE_VMEM)
    own = jax.ShapeDtypeStruct((tok, OWN_COLS), bf16)
    early = jax.ShapeDtypeStruct((nodes, page_tok, KV_COLS), bf16)
    late = jax.ShapeDtypeStruct((page_tok, KV_COLS), bf16)
    owner_of, slot_of = page_owner.T, page_slot.T
    send, picks = pl.pallas_call(
        stage_kernel,
        in_specs=[hbm] * 5,
        out_specs=[vmem, smem],
        out_shape=[early, jax.ShapeDtypeStruct((segs,), i32)],
        scratch_shapes=[
            pltpu.SMEM(seg_parent.shape, i32),
            pltpu.SMEM(block_up.shape, i32),
            pltpu.VMEM(owner_of.shape, i32),
            pltpu.VMEM(slot_of.shape, i32),
            pltpu.SemaphoreType.DMA((5,)),
        ],
        compiler_params=wide,
        name="stage",
    )(seg_parent, block_up, owner_of, slot_of, kv_store)
    got = lax.all_to_all(send, "nodes", split_axis=0, concat_axis=0, tiled=True)
    bias, *staged = pl.pallas_call(
        pieces_kernel,
        in_specs=[smem] * 2 + [vmem] + [smem] + [hbm] * 3,
        out_specs=[vmem] * (1 + MEMBERS + nodes),
        out_shape=[jax.ShapeDtypeStruct((1, keys), f32)] + [own] * MEMBERS + [late] * nodes,
        scratch_shapes=[pltpu.SemaphoreType.DMA((MEMBERS + nodes,))],
        compiler_params=pltpu.CompilerParams(vmem_limit_bytes=PIECES_VMEM),
        name="pieces",
    )(seg_parent, block_up, owner_of, picks, queries, seg_kv, kv_store)
    owns, held = staged[:MEMBERS], staged[MEMBERS:]

    def swapped(x, d):
        return lax.ppermute(x, "nodes", [(i, i ^ d) for i in range(nodes)])

    pieces = [owns[0]] + [swapped(owns[d], d) for d in range(1, MEMBERS)]
    values = [held[0]] + [swapped(held[d], d) for d in range(1, nodes)]
    rows = GROUP * tok
    out_piece = jax.ShapeDtypeStruct((tok, GROUP * HEAD_DIM), bf16)
    sums = jax.ShapeDtypeStruct((MEMBERS, rows, HEAD_DIM), f32)
    results = pl.pallas_call(
        lambda *refs: weights_kernel(*refs),
        in_specs=[vmem] * (2 + MEMBERS),
        out_specs=[vmem] * (3 * HEADS_HERE),
        out_shape=[jax.ShapeDtypeStruct((MEMBERS, rows, keys), bf16), sums, sums] * HEADS_HERE,
        scratch_shapes=[pltpu.VMEM((rows, keys), f32)],
        compiler_params=params,
        name="weights",
    )(bias, *pieces, got)
    parts = []
    for h in range(HEADS_HERE):
        one = pl.pallas_call(
            lambda *refs, h=h: values_kernel(h, *refs),
            in_specs=[vmem] * (3 + nodes),
            out_specs=[vmem] * MEMBERS,
            out_shape=[out_piece] * MEMBERS,
            scratch_shapes=[pltpu.VMEM((keys, HEAD_DIM), bf16)],
            compiler_params=params,
        )(*results[3 * h : 3 * h + 3], *values)
        parts += [one[0]] + [swapped(one[d], d) for d in range(1, MEMBERS)]
    return pl.pallas_call(
        join_kernel,
        in_specs=[vmem] * 8,
        out_specs=hbm,
        out_shape=jax.ShapeDtypeStruct(queries.shape, bf16),
        scratch_shapes=[pltpu.SemaphoreType.DMA((8,))],
        compiler_params=params,
        name="join",
    )(*parts)


def solution(mesh):
    in_specs = (
        P(("groups", "nodes"), None),
        P(None, ("groups", "nodes"), None),
        P(None, ("groups", "nodes"), None, None),
        P("groups"),
        P("groups"),
        P("groups", None),
        P("groups", None),
    )
    out_specs = P(("groups", "nodes"), None)

    return jax.shard_map(local, mesh=mesh, in_specs=in_specs, out_specs=out_specs, check_vma=False)
```
